32 devices in a mesh: parts: 2 (over y), pool: 4 (over z), tp: 4 (over x, core).
Axes of the slice: x: 2, y: 2, z: 4, core: 2. Of those that a mesh axis runs over, the one named last changes fastest.
Arguments:
- queries: bfloat16 [4096, 8192], P(('parts', 'pool'), 'tp'), parts along dimension 0, may hold values from -400 to 400
- suffix_kv: bfloat16 [2, 8, 4096, 128], P(None, 'tp', ('parts', 'pool')), parts along dimension 2, may hold values from -12 to 12
- pool_kv: bfloat16 [2, 8, 64, 128, 128], P(None, 'tp', ('parts', 'pool')), parts along dimension 2, may hold values from -6 to 6
- prefix_pages: int32 [8], P('parts'), parts along dimension 0, may hold values from 1 to 4, as said below
- owner_start: int32 [8], P('parts'), parts along dimension 0, may hold values from 0 to 3
- page_slot: int32 [8, 4, 2], P('parts'), parts along dimension 0, may hold values from 0 to 7, as said below
Outputs:
- attention: bfloat16 [4096, 8192], P(('parts', 'pool'), 'tp'), parts along dimension 0
- new_pool: bfloat16 [2, 8, 64, 128, 128], P(None, 'tp', ('parts', 'pool')), parts along dimension 2
The draws below stay inside these ranges and needn't reach their ends.
There are 2 independent parts, one for each index of `parts`. The reference program is written for one: setup_inputs(seed, part) draws one part's arguments, and reference() takes and returns one part's arrays. A program takes and returns all parts, laid end to end along the dimension named above; each array names one. Nothing has to cross between parts.
Inputs may be any that keep to these rules, and one draw needn't show every extreme that they name: For each owner o, the entries page_slot[:, o, :] name each of its 8 slots exactly once. `prefix_pages`: among the 4 requests of one serving group, at least one has exactly 4 prefix pages.
All inputs are finite; a program needn't handle non-finite values.
Results may differ from the reference program's by a relative error of at most 0.0035.
Values may be sent and summed in bfloat16 or wider, within the bound.
A program may use at most 128 MiB of HBM per device.

```python
import math
import jax
import jax.numpy as jnp
from jax import lax

KVH = 8
HD = 128
GROUP = 8
PAGE = 128
CAP = 2
SUF = 512
REQS = 4
SLOTS = 8
MAXP = 8
SP = 4
POOL_PAGES = 32
N_POOL = 4


def joint_draw(key):
    base_key = jax.random.fold_in(key, 4242)
    key_query, key_cache = jax.random.split(base_key, 2)
    queries = jnp.clip(2.5 * jax.random.normal(key_query, (REQS * SUF, KVH * GROUP * HD), jnp.float32), -15.0, 15.0)
    cache = jnp.clip(jax.random.normal(key_cache, (2, KVH, REQS * SUF, HD), jnp.float32), -6.0, 6.0)
    return (queries, cache)


def draw_queries(key, part):
    return joint_draw(key)[0].astype(jnp.bfloat16)


def draw_suffix_kv(key, part):
    return joint_draw(key)[1].astype(jnp.bfloat16)


def draw_prefix_pages(key, part):
    length_key, pick_key = jax.random.split(jax.random.fold_in(key, 517))
    longest = MAXP - SP
    lengths = jax.random.randint(length_key, (REQS,), 1, longest + 1, dtype=jnp.int32)
    chosen = jax.random.randint(pick_key, (), 0, REQS, dtype=jnp.int32)
    places = jnp.arange(REQS, dtype=jnp.int32)
    return jnp.where(places == chosen, longest, lengths).astype(jnp.int32)


def owner_order(owner_key):
    return jax.random.permutation(owner_key, REQS * CAP).astype(jnp.int32)


def draw_page_slot(key, part):
    owner_keys = jax.random.split(jax.random.fold_in(key, 99), N_POOL)
    orders = jax.vmap(owner_order)(owner_keys).reshape(N_POOL, REQS, CAP)
    return jnp.transpose(orders, (1, 0, 2)).astype(jnp.int32)


def plant(array, rng, low, top_value):
    spot = [jax.random.randint(jax.random.fold_in(rng, axis), (), 0, length) for axis, length in enumerate(array.shape)]
    main_axis = array.shape.index(max(array.shape))
    neighbour = spot[:main_axis] + [(spot[main_axis] + 1) % array.shape[main_axis]] + spot[main_axis + 1:]
    return array.at[tuple(spot)].set(low).at[tuple(neighbour)].set(top_value)


def block_scale(rng, extent, cuts, smallest, largest):
    def one(position, parts):
        steps = jax.random.uniform(jax.random.fold_in(jax.random.fold_in(rng, 6), position), (parts,), jnp.float32, smallest / len(cuts), largest / len(cuts))
        return jnp.repeat(jnp.exp(steps), extent[position] // parts).reshape((-1,) + (1,) * (len(extent) - position - 1))

    gain = one(*cuts[0])
    for cut in cuts[1:]:
        gain = gain * one(*cut)
    return gain


def noise(own_key, extent, width, limit, pieces=(), kind=jnp.bfloat16):
    result = width * jax.random.normal(own_key, extent, jnp.float32)
    if pieces:
        result = result * block_scale(own_key, extent, pieces, -0.22, 0.18)
    return jnp.clip(result, -limit, limit).astype(kind)


def setup_inputs(seed: int = 0, part: int = 0) -> dict:
    key_of = jax.random.split(jax.random.key(seed), 7)
    own_keys = jax.random.split(jax.random.fold_in(key_of[6], part), 7)
    queries = draw_queries(jax.random.fold_in(jax.random.fold_in(key_of[6], part), 71), part)
    suffix_kv = draw_suffix_kv(jax.random.fold_in(jax.random.fold_in(key_of[6], part), 71), part)
    pool_kv = noise(own_keys[2], (2, KVH, POOL_PAGES, PAGE, HD), 1.0, 6.0, ((1, 4), (2, 4)))
    prefix_pages = draw_prefix_pages(jax.random.fold_in(jax.random.fold_in(key_of[6], part), 71), part)
    owner_start = plant(jax.random.randint(own_keys[4], (REQS,), 0, N_POOL), jax.random.fold_in(own_keys[4], 1), 0, N_POOL - 1).astype(jnp.int32)
    page_slot = draw_page_slot(jax.random.fold_in(jax.random.fold_in(key_of[6], part), 71), part)
    return dict(queries=queries, suffix_kv=suffix_kv, pool_kv=pool_kv, prefix_pages=prefix_pages, owner_start=owner_start, page_slot=page_slot)


def page_rows(prefix_pages, owner_start, page_slot):
    numbers = jnp.arange(MAXP, dtype=jnp.int32)
    owner_ids = jnp.mod(owner_start[:, None] + numbers[None, :], N_POOL).astype(jnp.int32)
    level_ids = jnp.broadcast_to(numbers[None, :] // N_POOL, owner_ids.shape)
    request_ids = jnp.broadcast_to(jnp.arange(REQS, dtype=jnp.int32)[:, None], owner_ids.shape)
    return (owner_ids * SLOTS + page_slot[request_ids, owner_ids, level_ids]).astype(jnp.int32)

def reference(queries, suffix_kv, pool_kv, prefix_pages, owner_start, page_slot):
    rows_table = page_rows(prefix_pages, owner_start, page_slot)
    score_scale = 1.0 / math.sqrt(HD)
    page_ids = jnp.arange(MAXP * PAGE, dtype=jnp.int32) // PAGE
    causal = lax.broadcasted_iota(jnp.int32, (SUF, SUF), 1) <= lax.broadcasted_iota(jnp.int32, (SUF, SUF), 0)

    def per_request(request):
        gathered = jnp.take(pool_kv, rows_table[request], axis=2)
        prefix_rows = gathered.reshape(2, KVH, MAXP * PAGE, HD)
        own_rows = lax.dynamic_slice_in_dim(suffix_kv, (request * SUF).astype(jnp.int32), SUF, 2)
        context = jnp.concatenate([prefix_rows, own_rows], axis=2)
        query_rows = lax.dynamic_slice_in_dim(queries, (request * SUF).astype(jnp.int32), SUF, 0)
        query_rows = query_rows.reshape(SUF, KVH, GROUP, HD)
        prefix_seen = page_ids < prefix_pages[request]
        visible = jnp.concatenate([jnp.broadcast_to(prefix_seen[None, :], (SUF, MAXP * PAGE)), causal], axis=1)

        def per_head(kv_head):
            pair = lax.dynamic_index_in_dim(context, kv_head, 1, keepdims=False)
            key_rows = pair[0].astype(jnp.float32)
            value_rows = pair[1].astype(jnp.float32)
            heads_query = lax.dynamic_index_in_dim(query_rows, kv_head, 1, keepdims=False).astype(jnp.float32)
            scores = jnp.einsum('qgd,kd->gqk', heads_query, key_rows) * score_scale
            scores = jnp.where(visible[None], scores, -jnp.inf)
            row_max = lax.optimization_barrier(jnp.max(scores, axis=-1, keepdims=True))
            weights = jnp.exp(scores - row_max)
            weight_sum = lax.optimization_barrier(jnp.sum(weights, axis=-1))
            rounded = lax.optimization_barrier(weights.astype(jnp.bfloat16)).astype(jnp.float32)
            mixed_rows = jnp.einsum('gqk,kd->qgd', rounded, value_rows)
            return mixed_rows / jnp.transpose(weight_sum)[:, :, None]
        heads_out = lax.map(per_head, jnp.arange(KVH, dtype=jnp.int32))
        return jnp.transpose(heads_out, (1, 0, 2, 3)).reshape(SUF, KVH * GROUP * HD).astype(jnp.bfloat16)
    attention = lax.map(per_request, jnp.arange(REQS, dtype=jnp.int32)).reshape(REQS * SUF, KVH * GROUP * HD)
    offsets = jnp.arange(SP, dtype=jnp.int32)
    numbers = prefix_pages[:, None] + offsets[None, :]
    owner_ids = jnp.mod(owner_start[:, None] + numbers, N_POOL).astype(jnp.int32)
    request_ids = jnp.broadcast_to(jnp.arange(REQS, dtype=jnp.int32)[:, None], owner_ids.shape)
    targets = owner_ids * SLOTS + page_slot[request_ids, owner_ids, numbers // N_POOL]
    fresh_pages = suffix_kv.reshape(2, KVH, REQS * SP, PAGE, HD)
    new_pool = pool_kv.at[:, :, targets.reshape(-1).astype(jnp.int32)].set(fresh_pages)
    return (attention, new_pool)
```

```python
import functools
import math

import jax
import jax.numpy as jnp
from jax import lax
from jax.experimental import pallas as pl
from jax.experimental.pallas import tpu as pltpu
from jax.sharding import PartitionSpec as P

NT = (((1,), (1,)), ((), ()))
ROWS = 128
KEY_BLOCK = 512


def kernel(
    groups,
    prefix_levels,
    length_ref,
    start_ref,
    slot_ref,
    q_ref,
    own_ref,
    pool_ref,
    out_ref,
    new_ref,
    send,
    recv,
    back_send,
    back_recv,
    own_values,
    page_keys,
    page_values,
    acc,
    top,
    send_sem,
    recv_sem,
    back_send_sem,
    back_recv_sem,
):
    me = lax.axis_index("pool")
    local_heads = pool_ref.shape[1]
    slot_count = pool_ref.shape[2]
    page_len = pool_ref.shape[3]
    dim = pool_ref.shape[4]
    levels = slot_ref.shape[1]
    suffix = q_ref.shape[0]
    heads = q_ref.shape[1] // dim
    per_kv = heads // local_heads
    suffix_pages = suffix // page_len
    factor = math.log2(math.e) / math.sqrt(dim)
    rows = min(ROWS, suffix)

    def wrap(value):
        return lax.rem(value + groups * (levels + 1), groups)

    barrier = pltpu.get_barrier_semaphore()
    for step in range(1, groups):
        pl.semaphore_signal(
            barrier,
            inc=1,
            device_id={"pool": lax.rem(me + step, groups)},
            device_id_type=pl.DeviceIdType.MESH,
        )

    my_start = start_ref[me]
    my_length = length_ref[me]
    for level in range(prefix_levels):
        for step in range(groups):
            request = lax.rem(me + step, groups)
            page = pool_ref[:, :, slot_ref[request, level, me]]
            if step:
                send[level * groups + step] = page
            else:
                recv[level * groups] = page
    for step in range(groups):
        offset = wrap(me + step - my_start - my_length)
        offset = jnp.minimum(offset, suffix_pages - 1)
        page = own_ref[:, :, offset]
        if step:
            back_send[step] = page
        else:
            back_recv[0] = page
    for head in range(local_heads):
        own_values[head, :, :dim] = own_ref[1, head].reshape(suffix, dim)
        own_values[head, :, dim:] = jnp.ones((suffix, dim), jnp.bfloat16)

    pl.semaphore_wait(barrier, groups - 1)
    copies = []
    back_copies = []
    for level in range(prefix_levels):
        for step in range(1, groups):
            place = level * groups + step
            copy = pltpu.make_async_remote_copy(
                src_ref=send.at[place],
                dst_ref=recv.at[place],
                send_sem=send_sem.at[place],
                recv_sem=recv_sem.at[place],
                device_id={"pool": lax.rem(me + step, groups)},
                device_id_type=pl.DeviceIdType.MESH,
            )
            copy.start()
            copies.append(copy)
    for step in range(1, groups):
        copy = pltpu.make_async_remote_copy(
            src_ref=back_send.at[step],
            dst_ref=back_recv.at[step],
            send_sem=back_send_sem.at[step],
            recv_sem=back_recv_sem.at[step],
            device_id={"pool": lax.rem(me + step, groups)},
            device_id_type=pl.DeviceIdType.MESH,
        )
        copy.start()
        back_copies.append(copy)

    causal = lax.broadcasted_iota(jnp.int32, (rows, rows), 1) <= lax.broadcasted_iota(
        jnp.int32, (rows, rows), 0
    )

    def own_step(head, carry):
        kv_head = head // per_kv
        columns = pl.ds(pl.multiple_of(head * dim, dim), dim)
        for first in range(0, suffix, rows):
            end = first + rows
            scores = lax.dot_general(
                q_ref[first:end, columns],
                own_ref[0, kv_head, : end // page_len].reshape(end, dim),
                NT,
                preferred_element_type=jnp.float32,
            )
            last = jnp.where(causal, scores[:, first:], -jnp.inf)
            scores = jnp.concatenate([scores[:, :first], last], axis=1) if first else last
            highest = jnp.max(scores, axis=1, keepdims=True)
            weights = jnp.exp2((scores - highest) * factor).astype(jnp.bfloat16)
            acc[head, first:end] = jnp.dot(
                weights, own_values[kv_head, :end], preferred_element_type=jnp.float32
            )
            top[head, first:end] = jnp.broadcast_to(highest, (rows, dim))
        return carry

    lax.fori_loop(0, heads, own_step, 0)

    for copy in copies:
        copy.wait()
    first_page = wrap(me - my_start)
    for level in range(prefix_levels):
        for step in range(groups):
            place = level * groups + step
            number = level * groups + wrap(me - step - my_start)
            live = number < my_length
            source = jnp.where(live, place, first_page)
            keep = live.astype(jnp.float32)
            span = slice(place * page_len, (place + 1) * page_len)
            for head in range(local_heads):
                page_keys[head, span] = recv[source, 0, head]
                page_values[head, span, :dim] = (
                    recv[place, 1, head].astype(jnp.float32) * keep
                ).astype(jnp.bfloat16)
                page_values[head, span, dim:] = jnp.full(
                    (page_len, dim), keep, jnp.float32
                ).astype(jnp.bfloat16)

    total = prefix_levels * groups * page_len
    block = min(KEY_BLOCK, total)

    def page_step(head, carry):
        kv_head = head // per_kv
        columns = pl.ds(pl.multiple_of(head * dim, dim), dim)
        for first in range(0, suffix, rows):
            end = first + rows
            mixed = acc[head, first:end]
            highest = top[head, first:end]
            for key_first in range(0, total, block):
                width = min(block, total - key_first)
                scores = lax.dot_general(
                    q_ref[first:end, columns],
                    page_keys[kv_head, key_first : key_first + width],
                    NT,
                    preferred_element_type=jnp.float32,
                )
                risen = jnp.maximum(highest, jnp.max(scores, axis=1, keepdims=True))
                shrink = jnp.exp2((highest - risen) * factor)
                weights = jnp.concatenate(
                    [
                        jnp.exp2((scores[:, at : at + dim] - risen) * factor).astype(jnp.bfloat16)
                        for at in range(0, width, dim)
                    ],
                    axis=1,
                )
                mixed = mixed * jnp.concatenate([shrink, shrink], axis=1) + jnp.dot(
                    weights,
                    page_values[kv_head, key_first : key_first + width],
                    preferred_element_type=jnp.float32,
                )
                highest = risen
            out_ref[first:end, columns] = (mixed[:, :dim] / mixed[:, dim:]).astype(jnp.bfloat16)
        return carry

    lax.fori_loop(0, heads, page_step, 0)

    for copy in back_copies:
        copy.wait()
    targets = []
    for step in range(groups):
        request = lax.rem(me - step + groups, groups)
        offset = wrap(me - start_ref[request] - length_ref[request])
        level = jnp.minimum((length_ref[request] + offset) // groups, levels - 1)
        target = slot_ref[request, level, me]
        targets.append(jnp.where(offset < suffix_pages, target, slot_count))

    def slot_step(slot, carry):
        chosen = jnp.int32(0)
        hit = jnp.int32(0)
        for step in range(groups):
            match = targets[step] == slot
            chosen = jnp.where(match, step, chosen)
            hit = jnp.where(match, 1, hit)
        taken = jnp.full((page_len, dim), hit, jnp.int32) > 0
        for which in range(2):
            for head in range(local_heads):
                fresh = back_recv[chosen, which, head].astype(jnp.float32)
                old = pool_ref[which, head, slot].astype(jnp.float32)
                new_ref[which, head, slot] = jnp.where(taken, fresh, old).astype(jnp.bfloat16)
        return carry

    lax.fori_loop(0, slot_count, slot_step, 0)


def body(queries, suffix_kv, pool_kv, prefix_pages, owner_start, page_slot):
    groups = lax.axis_size("pool")
    _, local_heads, slot_count, page_len, dim = pool_kv.shape
    levels = page_slot.shape[2]
    suffix, width = queries.shape
    heads = width // dim
    suffix_pages = suffix // page_len
    prefix_levels = max(1, -(-(groups * levels - suffix_pages) // groups))
    pages = prefix_levels * groups
    page_shape = (2, local_heads, page_len, dim)
    smem = pl.BlockSpec(memory_space=pltpu.SMEM)
    vmem = pl.BlockSpec(memory_space=pltpu.VMEM)
    bf16 = jnp.bfloat16
    return pl.pallas_call(
        functools.partial(kernel, groups, prefix_levels),
        out_shape=(
            jax.ShapeDtypeStruct(queries.shape, bf16),
            jax.ShapeDtypeStruct(pool_kv.shape, bf16),
        ),
        in_specs=[smem, smem, smem, vmem, vmem, vmem],
        out_specs=(vmem, vmem),
        scratch_shapes=[
            pltpu.VMEM((pages,) + page_shape, bf16),
            pltpu.VMEM((pages,) + page_shape, bf16),
            pltpu.VMEM((groups,) + page_shape, bf16),
            pltpu.VMEM((groups,) + page_shape, bf16),
            pltpu.VMEM((local_heads, suffix, 2 * dim), bf16),
            pltpu.VMEM((local_heads, pages * page_len, dim), bf16),
            pltpu.VMEM((local_heads, pages * page_len, 2 * dim), bf16),
            pltpu.VMEM((heads, suffix, 2 * dim), jnp.float32),
            pltpu.VMEM((heads, suffix, dim), jnp.float32),
            pltpu.SemaphoreType.DMA((pages,)),
            pltpu.SemaphoreType.DMA((pages,)),
            pltpu.SemaphoreType.DMA((groups,)),
            pltpu.SemaphoreType.DMA((groups,)),
        ],
        compiler_params=pltpu.CompilerParams(
            collective_id=0, has_side_effects=True, vmem_limit_bytes=56 * 1024 * 1024
        ),
    )(
        prefix_pages,
        owner_start,
        jnp.transpose(page_slot, (0, 2, 1)),
        queries,
        suffix_kv.reshape(2, local_heads, suffix_pages, page_len, dim),
        pool_kv,
    )


def solution(mesh):
    in_specs = (
        P(("parts", "pool"), "tp"),
        P(None, "tp", ("parts", "pool"), None),
        P(None, "tp", ("parts", "pool"), None, None),
        P("parts"),
        P("parts"),
        P("parts", None, None),
    )
    out_specs = (P(("parts", "pool"), "tp"), P(None, "tp", ("parts", "pool"), None, None))
    return jax.shard_map(body, mesh=mesh, in_specs=in_specs, out_specs=out_specs, check_vma=False)
```

```python
import functools
import math

import jax
import jax.numpy as jnp
from jax import lax
from jax.experimental import pallas as pl
from jax.experimental.pallas import tpu as pltpu
from jax.sharding import PartitionSpec as P

NT = (((1,), (1,)), ((), ()))
ROWS = 256
KEY_BLOCK = 512


def kernel(
    groups,
    prefix_levels,
    length_ref,
    start_ref,
    slot_ref,
    q_ref,
    own_ref,
    pool_ref,
    out_ref,
    new_ref,
    send,
    recv,
    back_send,
    back_recv,
    own_values,
    page_keys,
    page_values,
    acc,
    top,
    send_sem,
    recv_sem,
    back_send_sem,
    back_recv_sem,
):
    me = lax.axis_index("pool")
    local_heads = pool_ref.shape[1]
    slot_count = pool_ref.shape[2]
    page_len = pool_ref.shape[3]
    dim = pool_ref.shape[4]
    levels = slot_ref.shape[1]
    suffix = q_ref.shape[0]
    heads = q_ref.shape[1] // dim
    per_kv = heads // local_heads
    suffix_pages = suffix // page_len
    factor = math.log2(math.e) / math.sqrt(dim)
    rows = min(ROWS, suffix)

    def wrap(value):
        return lax.rem(value + groups * (levels + 1), groups)

    barrier = pltpu.get_barrier_semaphore()
    for step in range(1, groups):
        pl.semaphore_signal(
            barrier,
            inc=1,
            device_id={"pool": lax.rem(me + step, groups)},
            device_id_type=pl.DeviceIdType.MESH,
        )

    my_start = start_ref[me]
    my_length = length_ref[me]
    for level in range(prefix_levels):
        for step in range(groups):
            request = lax.rem(me + step, groups)
            page = pool_ref[:, :, slot_ref[request, level, me]]
            if step:
                send[level * groups + step] = page
            else:
                recv[level * groups] = page
    for step in range(groups):
        offset = wrap(me + step - my_start - my_length)
        offset = jnp.minimum(offset, suffix_pages - 1)
        page = own_ref[:, :, offset]
        if step:
            back_send[step] = page
        else:
            back_recv[0] = page
    for head in range(local_heads):
        own_values[head, :, :dim] = own_ref[1, head].reshape(suffix, dim)
        own_values[head, :, dim:] = jnp.ones((suffix, dim), jnp.bfloat16)

    pl.semaphore_wait(barrier, groups - 1)
    copies = []
    back_copies = []
    for level in range(prefix_levels):
        for step in range(1, groups):
            place = level * groups + step
            copy = pltpu.make_async_remote_copy(
                src_ref=send.at[place],
                dst_ref=recv.at[place],
                send_sem=send_sem.at[place],
                recv_sem=recv_sem.at[place],
                device_id={"pool": lax.rem(me + step, groups)},
                device_id_type=pl.DeviceIdType.MESH,
            )
            copy.start()
            copies.append(copy)
    masks = {}
    for at in range(0, rows, dim):
        masks[at] = lax.broadcasted_iota(jnp.int32, (rows, dim), 1) + at <= lax.broadcasted_iota(
            jnp.int32, (rows, dim), 0
        )

    def own_step(head, carry):
        kv_head = head // per_kv
        columns = pl.ds(pl.multiple_of(head * dim, dim), dim)
        for first in range(0, suffix, rows):
            end = first + rows
            scores = lax.dot_general(
                q_ref[first:end, columns],
                own_ref[0, kv_head, : end // page_len].reshape(end, dim),
                NT,
                preferred_element_type=jnp.float32,
            )
            pieces = []
            for at in range(0, end, dim):
                piece = scores[:, at : at + dim]
                if at + dim > first + 1:
                    piece = jnp.where(masks[at - first], piece, -jnp.inf)
                pieces.append(piece)
            peak = functools.reduce(jnp.maximum, pieces)
            highest = jnp.broadcast_to(jnp.max(peak, axis=1, keepdims=True), (rows, dim))
            weights = jnp.concatenate(
                [jnp.exp2((piece - highest) * factor).astype(jnp.bfloat16) for piece in pieces], axis=1
            )
            acc[head, first:end] = jnp.dot(
                weights, own_values[kv_head, :end], preferred_element_type=jnp.float32
            )
            top[head, first:end] = highest
        return carry

    lax.fori_loop(0, heads, own_step, 0, unroll=4)

    for copy in copies:
        copy.wait()
    for step in range(1, groups):
        copy = pltpu.make_async_remote_copy(
            src_ref=back_send.at[step],
            dst_ref=back_recv.at[step],
            send_sem=back_send_sem.at[step],
            recv_sem=back_recv_sem.at[step],
            device_id={"pool": lax.rem(me + step, groups)},
            device_id_type=pl.DeviceIdType.MESH,
        )
        copy.start()
        back_copies.append(copy)
    first_page = wrap(me - my_start)
    for level in range(prefix_levels):
        for step in range(groups):
            place = level * groups + step
            number = level * groups + wrap(me - step - my_start)
            live = number < my_length
            source = jnp.where(live, place, first_page)
            keep = live.astype(jnp.float32)
            span = slice(place * page_len, (place + 1) * page_len)
            for head in range(local_heads):
                page_keys[head, span] = recv[source, 0, head]
                page_values[head, span, :dim] = (
                    recv[place, 1, head].astype(jnp.float32) * keep
                ).astype(jnp.bfloat16)
                page_values[head, span, dim:] = jnp.full(
                    (page_len, dim), keep, jnp.float32
                ).astype(jnp.bfloat16)

    total = prefix_levels * groups * page_len
    block = min(KEY_BLOCK, total)

    def page_step(head, carry):
        kv_head = head // per_kv
        columns = pl.ds(pl.multiple_of(head * dim, dim), dim)
        for first in range(0, suffix, rows):
            end = first + rows
            mixed = acc[head, first:end]
            highest = top[head, first:end]
            for key_first in range(0, total, block):
                width = min(block, total - key_first)
                scores = lax.dot_general(
                    q_ref[first:end, columns],
                    page_keys[kv_head, key_first : key_first + width],
                    NT,
                    preferred_element_type=jnp.float32,
                )
                risen = jnp.maximum(highest, jnp.max(scores, axis=1, keepdims=True))
                shrink = jnp.exp2((highest - risen) * factor)
                weights = jnp.concatenate(
                    [
                        jnp.exp2((scores[:, at : at + dim] - risen) * factor).astype(jnp.bfloat16)
                        for at in range(0, width, dim)
                    ],
                    axis=1,
                )
                mixed = mixed * jnp.concatenate([shrink, shrink], axis=1) + jnp.dot(
                    weights,
                    page_values[kv_head, key_first : key_first + width],
                    preferred_element_type=jnp.float32,
                )
                highest = risen
            out_ref[first:end, columns] = (mixed[:, :dim] / mixed[:, dim:]).astype(jnp.bfloat16)
        return carry

    lax.fori_loop(0, heads, page_step, 0, unroll=4)

    for copy in back_copies:
        copy.wait()
    targets = []
    for step in range(groups):
        request = lax.rem(me - step + groups, groups)
        offset = wrap(me - start_ref[request] - length_ref[request])
        level = jnp.minimum((length_ref[request] + offset) // groups, levels - 1)
        target = slot_ref[request, level, me]
        targets.append(jnp.where(offset < suffix_pages, target, slot_count))

    def slot_step(slot, carry):
        chosen = jnp.int32(0)
        hit = jnp.int32(0)
        for step in range(groups):
            match = targets[step] == slot
            chosen = jnp.where(match, step, chosen)
            hit = jnp.where(match, 1, hit)
        taken = jnp.full((page_len, dim), hit, jnp.int32) > 0
        for which in range(2):
            for head in range(local_heads):
                fresh = back_recv[chosen, which, head].astype(jnp.float32)
                old = pool_ref[which, head, slot].astype(jnp.float32)
                new_ref[which, head, slot] = jnp.where(taken, fresh, old).astype(jnp.bfloat16)
        return carry

    lax.fori_loop(0, slot_count, slot_step, 0)


def body(queries, suffix_kv, pool_kv, prefix_pages, owner_start, page_slot):
    groups = lax.axis_size("pool")
    _, local_heads, slot_count, page_len, dim = pool_kv.shape
    levels = page_slot.shape[2]
    suffix, width = queries.shape
    heads = width // dim
    suffix_pages = suffix // page_len
    prefix_levels = max(1, -(-(groups * levels - suffix_pages) // groups))
    pages = prefix_levels * groups
    page_shape = (2, local_heads, page_len, dim)
    smem = pl.BlockSpec(memory_space=pltpu.SMEM)
    vmem = pl.BlockSpec(memory_space=pltpu.VMEM)
    bf16 = jnp.bfloat16
    return pl.pallas_call(
        functools.partial(kernel, groups, prefix_levels),
        out_shape=(
            jax.ShapeDtypeStruct(queries.shape, bf16),
            jax.ShapeDtypeStruct(pool_kv.shape, bf16),
        ),
        in_specs=[smem, smem, smem, vmem, vmem, vmem],
        out_specs=(vmem, vmem),
        scratch_shapes=[
            pltpu.VMEM((pages,) + page_shape, bf16),
            pltpu.VMEM((pages,) + page_shape, bf16),
            pltpu.VMEM((groups,) + page_shape, bf16),
            pltpu.VMEM((groups,) + page_shape, bf16),
            pltpu.VMEM((local_heads, suffix, 2 * dim), bf16),
            pltpu.VMEM((local_heads, pages * page_len, dim), bf16),
            pltpu.VMEM((local_heads, pages * page_len, 2 * dim), bf16),
            pltpu.VMEM((heads, suffix, 2 * dim), jnp.float32),
            pltpu.VMEM((heads, suffix, dim), jnp.float32),
            pltpu.SemaphoreType.DMA((pages,)),
            pltpu.SemaphoreType.DMA((pages,)),
            pltpu.SemaphoreType.DMA((groups,)),
            pltpu.SemaphoreType.DMA((groups,)),
        ],
        compiler_params=pltpu.CompilerParams(
            collective_id=0, has_side_effects=True, vmem_limit_bytes=56 * 1024 * 1024
        ),
    )(
        prefix_pages,
        owner_start,
        jnp.transpose(page_slot, (0, 2, 1)),
        queries,
        suffix_kv.reshape(2, local_heads, suffix_pages, page_len, dim),
        pool_kv,
    )


def solution(mesh):
    in_specs = (
        P(("parts", "pool"), "tp"),
        P(None, "tp", ("parts", "pool"), None),
        P(None, "tp", ("parts", "pool"), None, None),
        P("parts"),
        P("parts"),
        P("parts", None, None),
    )
    out_specs = (P(("parts", "pool"), "tp"), P(None, "tp", ("parts", "pool"), None, None))
    return jax.shard_map(body, mesh=mesh, in_specs=in_specs, out_specs=out_specs, check_vma=False)
```

```python
import functools
import math

import jax
import jax.numpy as jnp
from jax import lax
from jax.experimental import pallas as pl
from jax.experimental.pallas import tpu as pltpu
from jax.sharding import PartitionSpec as P

NT = (((1,), (1,)), ((), ()))
ROWS = 256
KEY_BLOCK = 512


def kernel(
    groups,
    prefix_levels,
    length_ref,
    start_ref,
    slot_ref,
    q_hbm,
    own_ref,
    pool_ref,
    out_hbm,
    back_recv,
    q_ref,
    out_ref,
    q_sem,
    out_sem,
    send,
    recv,
    back_send,
    own_values,
    page_keys,
    page_values,
    acc,
    top,
    send_sem,
    recv_sem,
    back_send_sem,
    back_recv_sem,
):
    q_load = pltpu.make_async_copy(q_hbm, q_ref, q_sem)
    q_load.start()
    me = lax.axis_index("pool")
    local_heads = pool_ref.shape[1]
    slot_count = pool_ref.shape[2]
    page_len = pool_ref.shape[3]
    dim = pool_ref.shape[4]
    levels = slot_ref.shape[1]
    suffix = q_ref.shape[0]
    heads = q_ref.shape[1] // dim
    per_kv = heads // local_heads
    suffix_pages = suffix // page_len
    factor = math.log2(math.e) / math.sqrt(dim)
    rows = min(ROWS, suffix)

    def wrap(value):
        return lax.rem(value + groups * (levels + 1), groups)

    barrier = pltpu.get_barrier_semaphore()
    for step in range(1, groups):
        pl.semaphore_signal(
            barrier,
            inc=1,
            device_id={"pool": lax.rem(me + step, groups)},
            device_id_type=pl.DeviceIdType.MESH,
        )

    my_start = start_ref[me]
    my_length = length_ref[me]
    for level in range(prefix_levels):
        for step in range(groups):
            request = lax.rem(me + step, groups)
            page = pool_ref[:, :, slot_ref[request, level, me]]
            if step:
                send[level * groups + step] = page
            else:
                recv[level * groups] = page
    for step in range(groups):
        offset = wrap(me + step - my_start - my_length)
        offset = jnp.minimum(offset, suffix_pages - 1)
        page = own_ref[:, :, offset]
        if step:
            back_send[step] = page
        else:
            back_recv[0] = page
    for head in range(local_heads):
        own_values[head, :, :dim] = own_ref[1, head].reshape(suffix, dim)
        own_values[head, :, dim:] = jnp.ones((suffix, dim), jnp.bfloat16)

    pl.semaphore_wait(barrier, groups - 1)
    copies = []
    back_copies = []
    for level in range(prefix_levels):
        for step in range(1, groups):
            place = level * groups + step
            copy = pltpu.make_async_remote_copy(
                src_ref=send.at[place],
                dst_ref=recv.at[place],
                send_sem=send_sem.at[place],
                recv_sem=recv_sem.at[place],
                device_id={"pool": lax.rem(me + step, groups)},
                device_id_type=pl.DeviceIdType.MESH,
            )
            copy.start()
            copies.append(copy)
    masks = {}
    for at in range(0, rows, dim):
        masks[at] = lax.broadcasted_iota(jnp.int32, (rows, dim), 1) + at <= lax.broadcasted_iota(
            jnp.int32, (rows, dim), 0
        )

    def own_step(head, carry):
        kv_head = head // per_kv
        columns = pl.ds(pl.multiple_of(head * dim, dim), dim)
        for first in range(0, suffix, rows):
            end = first + rows
            scores = lax.dot_general(
                q_ref[first:end, columns],
                own_ref[0, kv_head, : end // page_len].reshape(end, dim),
                NT,
                preferred_element_type=jnp.float32,
            )
            pieces = []
            for at in range(0, end, dim):
                piece = scores[:, at : at + dim]
                if at + dim > first + 1:
                    piece = jnp.where(masks[at - first], piece, -jnp.inf)
                pieces.append(piece)
            peak = functools.reduce(jnp.maximum, pieces)
            highest = jnp.broadcast_to(jnp.max(peak, axis=1, keepdims=True), (rows, dim))
            weights = jnp.concatenate(
                [jnp.exp2((piece - highest) * factor).astype(jnp.bfloat16) for piece in pieces], axis=1
            )
            acc[head, first:end] = jnp.dot(
                weights, own_values[kv_head, :end], preferred_element_type=jnp.float32
            )
            top[head, first:end] = highest
        return carry

    q_load.wait()
    lax.fori_loop(0, heads, own_step, 0, unroll=4)

    for copy in copies:
        copy.wait()
    for step in range(1, groups):
        copy = pltpu.make_async_remote_copy(
            src_ref=back_send.at[step],
            dst_ref=back_recv.at[step],
            send_sem=back_send_sem.at[step],
            recv_sem=back_recv_sem.at[step],
            device_id={"pool": lax.rem(me + step, groups)},
            device_id_type=pl.DeviceIdType.MESH,
        )
        copy.start()
        back_copies.append(copy)
    first_page = wrap(me - my_start)
    for level in range(prefix_levels):
        for step in range(groups):
            place = level * groups + step
            number = level * groups + wrap(me - step - my_start)
            live = number < my_length
            source = jnp.where(live, place, first_page)
            keep = live.astype(jnp.float32)
            span = slice(place * page_len, (place + 1) * page_len)
            for head in range(local_heads):
                page_keys[head, span] = recv[source, 0, head]
                page_values[head, span, :dim] = recv[place, 1, head] * keep.astype(jnp.bfloat16)
                page_values[head, span, dim:] = jnp.full(
                    (page_len, dim), keep, jnp.float32
                ).astype(jnp.bfloat16)

    total = prefix_levels * groups * page_len
    block = min(KEY_BLOCK, total)

    def store(head):
        columns = pl.ds(pl.multiple_of(head * dim, dim), dim)
        return pltpu.make_async_copy(out_ref.at[head], out_hbm.at[:, columns], out_sem.at[head])

    def page_step(head, carry):
        kv_head = head // per_kv
        columns = pl.ds(pl.multiple_of(head * dim, dim), dim)
        for first in range(0, suffix, rows):
            end = first + rows
            mixed = acc[head, first:end]
            highest = top[head, first:end]
            for key_first in range(0, total, block):
                width = min(block, total - key_first)
                scores = lax.dot_general(
                    q_ref[first:end, columns],
                    page_keys[kv_head, key_first : key_first + width],
                    NT,
                    preferred_element_type=jnp.float32,
                )
                risen = jnp.maximum(highest, jnp.max(scores, axis=1, keepdims=True))
                shrink = jnp.exp2((highest - risen) * factor)
                weights = jnp.concatenate(
                    [
                        jnp.exp2((scores[:, at : at + dim] - risen) * factor).astype(jnp.bfloat16)
                        for at in range(0, width, dim)
                    ],
                    axis=1,
                )
                mixed = mixed * jnp.concatenate([shrink, shrink], axis=1) + jnp.dot(
                    weights,
                    page_values[kv_head, key_first : key_first + width],
                    preferred_element_type=jnp.float32,
                )
                highest = risen
            out_ref[head, first:end] = (mixed[:, :dim] / mixed[:, dim:]).astype(jnp.bfloat16)
        store(head).start()
        return carry

    lax.fori_loop(0, heads, page_step, 0, unroll=4)

    def store_done(head, carry):
        store(head).wait()
        return carry

    lax.fori_loop(0, heads, store_done, 0)
    for copy in back_copies:
        copy.wait()


def finish(
    groups,
    length_ref,
    start_ref,
    slot_ref,
    mixed_ref,
    fresh_ref,
    pool_ref,
    out_ref,
    new_ref,
    mixed_buf,
    page_buf,
    mixed_in,
    mixed_out,
    page_in,
    page_out,
):
    me = lax.axis_index("pool")
    levels = slot_ref.shape[1]
    slot_count = pool_ref.shape[2]
    page_len = pool_ref.shape[3]
    suffix_pages = mixed_ref.shape[0] // page_len
    loads = []
    for part in range(suffix_pages):
        span = pl.ds(part * page_len, page_len)
        load = pltpu.make_async_copy(mixed_ref.at[span], mixed_buf.at[span], mixed_in.at[part])
        load.start()
        loads.append(load)
    targets = []
    for step in range(groups):
        request = lax.rem(me - step + groups, groups)
        length = length_ref[request]
        offset = lax.rem(me - start_ref[request] - length + groups * (levels + 1), groups)
        level = jnp.minimum((length + offset) // groups, levels - 1)
        target = slot_ref[request, level, me]
        targets.append(jnp.where(offset < suffix_pages, target, slot_count))
    page_loads = []
    for slot in range(slot_count):
        chosen = jnp.int32(0)
        hit = jnp.int32(0)
        for step in range(groups):
            match = targets[step] == slot
            chosen = jnp.where(match, step, chosen)
            hit = jnp.where(match, 1, hit)
        keep = pltpu.make_async_copy(pool_ref.at[:, :, slot], page_buf.at[slot], page_in.at[slot])
        swap = pltpu.make_async_copy(fresh_ref.at[chosen], page_buf.at[slot], page_in.at[slot])
        pl.when(hit == 0)(keep.start)
        pl.when(hit == 1)(swap.start)
        page_loads.append(keep)
    stores = []
    for part, load in enumerate(loads):
        load.wait()
        span = pl.ds(part * page_len, page_len)
        store = pltpu.make_async_copy(mixed_buf.at[span], out_ref.at[span], mixed_out.at[part])
        store.start()
        stores.append(store)
    for slot, load in enumerate(page_loads):
        load.wait()
        store = pltpu.make_async_copy(page_buf.at[slot], new_ref.at[:, :, slot], page_out.at[slot])
        store.start()
        stores.append(store)
    for store in stores:
        store.wait()


def body(queries, suffix_kv, pool_kv, prefix_pages, owner_start, page_slot):
    groups = lax.axis_size("pool")
    _, local_heads, slot_count, page_len, dim = pool_kv.shape
    levels = page_slot.shape[2]
    suffix, width = queries.shape
    heads = width // dim
    suffix_pages = suffix // page_len
    prefix_levels = max(1, -(-(groups * levels - suffix_pages) // groups))
    pages = prefix_levels * groups
    page_shape = (2, local_heads, page_len, dim)
    smem = pl.BlockSpec(memory_space=pltpu.SMEM)
    vmem = pl.BlockSpec(memory_space=pltpu.VMEM)
    bf16 = jnp.bfloat16
    anywhere = pl.BlockSpec(memory_space=pl.ANY)
    slots = jnp.transpose(page_slot, (0, 2, 1))
    mixed, fresh = pl.pallas_call(
        functools.partial(kernel, groups, prefix_levels),
        out_shape=(
            jax.ShapeDtypeStruct(queries.shape, bf16),
            jax.ShapeDtypeStruct((groups,) + page_shape, bf16),
        ),
        in_specs=[smem, smem, smem, anywhere, vmem, vmem],
        out_specs=(anywhere, vmem),
        scratch_shapes=[
            pltpu.VMEM(queries.shape, bf16),
            pltpu.VMEM((heads, suffix, dim), bf16),
            pltpu.SemaphoreType.DMA,
            pltpu.SemaphoreType.DMA((heads,)),
            pltpu.VMEM((pages,) + page_shape, bf16),
            pltpu.VMEM((pages,) + page_shape, bf16),
            pltpu.VMEM((groups,) + page_shape, bf16),
            pltpu.VMEM((local_heads, suffix, 2 * dim), bf16),
            pltpu.VMEM((local_heads, pages * page_len, dim), bf16),
            pltpu.VMEM((local_heads, pages * page_len, 2 * dim), bf16),
            pltpu.VMEM((heads, suffix, 2 * dim), jnp.float32),
            pltpu.VMEM((heads, suffix, dim), jnp.float32),
            pltpu.SemaphoreType.DMA((pages,)),
            pltpu.SemaphoreType.DMA((pages,)),
            pltpu.SemaphoreType.DMA((groups,)),
            pltpu.SemaphoreType.DMA((groups,)),
        ],
        compiler_params=pltpu.CompilerParams(
            collective_id=0, has_side_effects=True, vmem_limit_bytes=60 * 1024 * 1024
        ),
    )(
        prefix_pages,
        owner_start,
        slots,
        queries,
        suffix_kv.reshape(2, local_heads, suffix_pages, page_len, dim),
        pool_kv,
    )
    return pl.pallas_call(
        functools.partial(finish, groups),
        out_shape=(
            jax.ShapeDtypeStruct(queries.shape, bf16),
            jax.ShapeDtypeStruct(pool_kv.shape, bf16),
        ),
        in_specs=[smem, smem, smem, anywhere, anywhere, anywhere],
        out_specs=(anywhere, anywhere),
        scratch_shapes=[
            pltpu.VMEM(queries.shape, bf16),
            pltpu.VMEM((slot_count,) + page_shape, bf16),
            pltpu.SemaphoreType.DMA((suffix_pages,)),
            pltpu.SemaphoreType.DMA((suffix_pages,)),
            pltpu.SemaphoreType.DMA((slot_count,)),
            pltpu.SemaphoreType.DMA((slot_count,)),
        ],
        compiler_params=pltpu.CompilerParams(vmem_limit_bytes=60 * 1024 * 1024),
    )(prefix_pages, owner_start, slots, mixed, fresh, pool_kv)


def solution(mesh):
    in_specs = (
        P(("parts", "pool"), "tp"),
        P(None, "tp", ("parts", "pool"), None),
        P(None, "tp", ("parts", "pool"), None, None),
        P("parts"),
        P("parts"),
        P("parts", None, None),
    )
    out_specs = (P(("parts", "pool"), "tp"), P(None, "tp", ("parts", "pool"), None, None))
    return jax.shard_map(body, mesh=mesh, in_specs=in_specs, out_specs=out_specs, check_vma=False)
```
